1024 devices in a mesh: vel: 64 (over z_hi, x, core), space: 16 (over y, z_lo).
Axes of the slice: x: 8, y: 8, z: 8 (z_hi: 4, z_lo: 2; z = z_hi * 2 + z_lo), core: 2. Of those that a mesh axis runs over, the one named last changes fastest.
Arguments:
- distribution: float32 [1024, 256, 512], P('vel', 'space'), may hold values from -6 to 6
- courant: float32 [1024], replicated, may hold values from -0.9 to 0.9
- gain_matrix: bfloat16 [1024, 1024], replicated, may hold values from -0.1875 to 0.1875
- product_matrix: bfloat16 [1024, 1024], replicated, may hold values from -0.1875 to 0.1875
- collision_rate: float32 [256, 512], P('space'), may hold values from 0.5 to 2
Outputs:
- final_state: float32 [1024, 256, 512], P('vel', 'space')
The draws below stay inside these ranges and needn't reach their ends.
All inputs are finite; a program needn't handle non-finite values.
Results may differ from the reference program's by a relative error of at most 0.0016.
Values may be sent and summed in bfloat16 or wider, within the bound.
A program may use at most 64 MiB of HBM per device.

```python
import math
import jax
import jax.numpy as jnp
from jax import lax

V = 1024
PLANE = 512
STEPS = 2
NX = 256


def levels(stream_key, shape, shards, smallest, largest):
    loudness, own = 1.0, jax.random.fold_in(stream_key, 6)
    for axis_at, blocks in shards:
        heights = jnp.exp(jax.random.uniform(jax.random.fold_in(own, axis_at), (blocks,), jnp.float32, smallest / len(shards), largest / len(shards)))
        loudness = loudness * jnp.repeat(heights, shape[axis_at] // blocks).reshape([-1 if axis == axis_at else 1 for axis in range(len(shape))])
    return loudness


def centred(rng, shape, scale, limit, cuts=(), dtype=jnp.bfloat16):
    result = scale * jax.random.normal(rng, shape, jnp.float32)
    if cuts:
        result = result * levels(rng, shape, cuts, -0.22, 0.18)
    return jnp.clip(result, -limit, limit).astype(dtype)


def setup_inputs(seed: int = 0) -> dict:
    seeds = jax.random.split(jax.random.key(seed), 6)
    distribution = centred(seeds[0], (V, NX, PLANE), 1.0, 6.0, ((0, 64), (1, 16)), jnp.float32)
    courant = jnp.clip(jax.random.uniform(seeds[1], (V,), jnp.float32, -0.9, 0.9), -0.9, 0.9)
    gain_matrix = centred(seeds[2], (V, V), V ** -0.5, 0.1875)
    product_matrix = centred(seeds[3], (V, V), V ** -0.5, 0.1875)
    collision_rate = jnp.clip(jnp.exp(math.log(2.0) - 1.3862944 * jax.random.uniform(seeds[4], (NX, PLANE), jnp.float32) ** levels(seeds[4], (NX, PLANE), ((0, 16),), -0.2, 0.2)), 0.5, 2.0)
    return {"distribution": distribution, "courant": courant, "gain_matrix": gain_matrix, "product_matrix": product_matrix, "collision_rate": collision_rate}


time_step = 0.2


def minmod(first, second):
    return jnp.maximum(jnp.minimum(first, second), 0.0) + jnp.minimum(jnp.maximum(first, second), 0.0)


def change(widened, speeds):
    differ = widened[:, 1:] - widened[:, :-1]
    slopes = minmod(differ[:, 1:], differ[:, :-1])
    inner = widened.shape[1] - 4
    left_value = widened[:, 1:inner + 2]
    right_value = widened[:, 2:inner + 3]
    left_slope = slopes[:, 0:inner + 1]
    right_slope = slopes[:, 1:inner + 2]
    upward = jnp.maximum(speeds, 0.0)
    downward = jnp.minimum(speeds, 0.0)
    fluxes = upward * (left_value + 0.5 * (1.0 - speeds) * left_slope) + downward * (right_value - 0.5 * (1.0 + speeds) * right_slope)
    return -(fluxes[:, 1:] - fluxes[:, :-1])


def wrap_pad(field, width):
    return jnp.concatenate([field[:, -width:], field, field[:, :width]], axis=1)


def advect(field, speeds):
    section = field + change(wrap_pad(field, 2), speeds)
    return 0.5 * field + 0.5 * (section + change(wrap_pad(section, 2), speeds))


def collide(columns, gain_matrix, product_matrix):
    first_term = jnp.dot(gain_matrix, columns, preferred_element_type=jnp.float32)
    second_term = jnp.dot(product_matrix, columns, preferred_element_type=jnp.float32)
    return (first_term * second_term).astype(jnp.bfloat16)


def reference(distribution, courant, gain_matrix, product_matrix, collision_rate):
    state = distribution
    for step_index in range(STEPS):
        blocks = state.reshape(V // 16, 16, NX, PLANE)
        speed_blocks = courant.reshape(V // 16, 16, 1, 1)
        smoothed = lax.map(lambda pair: advect(pair[0], pair[1]), (blocks, speed_blocks)).reshape(V, NX, PLANE)
        rounded = smoothed.astype(jnp.bfloat16)
        planes = jnp.moveaxis(rounded, 1, 0)
        gains = lax.map(lambda plane_slice: collide(plane_slice, gain_matrix, product_matrix), planes)
        gained = jnp.moveaxis(gains, 0, 1)
        state = smoothed + time_step * (gained.astype(jnp.float32) - collision_rate[None] * rounded.astype(jnp.float32))
    return state
```

```python
import functools

import jax
import jax.numpy as jnp
from jax import lax
from jax.experimental import pallas as pl
from jax.experimental.pallas import tpu as pltpu
from jax.sharding import PartitionSpec as P

STEPS = 2
TIME_STEP = 0.2
MESH = pl.DeviceIdType.MESH
F32 = jnp.float32
BF16 = jnp.bfloat16
RING = 8
LANES = 128
GROUP = 16
PB = 8
SLAB = 32
HALO = 4
HALF = 512

OFFSETS = sorted(
    [(dx, dz) for dx in range(RING) for dz in range(RING) if (dx, dz) != (0, 0)],
    key=lambda o: -(min(o[0], RING - o[0]) + min(o[1], RING - o[1])),
)


def coords():
    vel, space = lax.axis_index("vel"), lax.axis_index("space")
    z_hi, x, core = vel // 16, (vel // 2) % 8, vel % 2
    y, z_lo = space // 2, space % 2
    return x, y, z_hi, z_lo, core


def device(x, y, z, core):
    return {"vel": (z // 2) * 16 + x * 2 + core, "space": y * 2 + z % 2}


def swap_groups(tiles):
    lane = lax.broadcasted_iota(jnp.int32, (8, LANES), 1) // GROUP
    tiles = list(tiles)
    for bit in (4, 2, 1):
        low = (lane & bit) == 0
        for i in range(8):
            if i & bit:
                continue
            j = i | bit
            a, b = tiles[i], tiles[j]
            tiles[i] = jnp.where(low, a, pltpu.roll(b, bit * GROUP, 1))
            tiles[j] = jnp.where(low, pltpu.roll(a, LANES - bit * GROUP, 1), b)
    return tiles


def minmod(a, b):
    return jnp.maximum(jnp.minimum(a, b), 0.0) + jnp.minimum(jnp.maximum(a, b), 0.0)


def sweep(values, up, down, ahead, behind):
    n = len(values)
    differ = [values[i + 1] - values[i] for i in range(n - 1)]
    slopes = [None] + [minmod(differ[i], differ[i - 1]) for i in range(1, n - 1)]
    fluxes = {}
    for i in range(1, n - 2):
        fluxes[i] = up * (values[i] + ahead * slopes[i]) + down * (
            values[i + 1] - behind * slopes[i + 1]
        )
    return {i: fluxes[i] - fluxes[i - 1] for i in range(2, n - 2)}


def kernel(
    dist_ref, cour_ref, gain_ref, prod_ref, rate_ref, out_ref,
    sin, send, recv, state, smooth, ownr, parr, halo, raw, turned, first, second,
    cour, rates, rate_cols, rate_b, sout, outr,
    in_sem, mat_sem, a2a_ss, a2a_rs, halo_ss, halo_rs, core_ss, core_rs,
    rate_sem, out_ss, out_rs,
):
    x, y, z_hi, z_lo, core = coords()
    z = z_hi * 2 + z_lo
    block = x * RING + z
    up_dev = device(x, lax.rem(y + 1, RING), z, core)
    down_dev = device(x, lax.rem(y + RING - 1, RING), z, core)
    twin = device(x, y, z, 1 - core)
    level = device(x, y, z_hi * 2 + 1 - z_lo, core)

    def far(o):
        return lax.rem(x + o[0], RING), lax.rem(z + o[1], RING)

    barrier = pltpu.get_barrier_semaphore()
    for o in OFFSETS:
        xx, zz = far(o)
        pl.semaphore_signal(barrier, 1, device_id=device(xx, y, zz, core), device_id_type=MESH)
    for peer in (up_dev, down_dev, twin):
        pl.semaphore_signal(barrier, 1, device_id=peer, device_id_type=MESH)

    load = pltpu.make_async_copy(dist_ref, sin, in_sem)
    load.start()
    mats = [
        pltpu.make_async_copy(gain_ref.at[:, core], raw.at[0], mat_sem.at[0]),
        pltpu.make_async_copy(prod_ref.at[:, core], raw.at[1], mat_sem.at[1]),
    ]
    for m in mats:
        m.start()
    load.wait()

    for h in range(2):
        for q in range(4):
            rows = jnp.concatenate(
                [sin[:, h * 8 + i, q * LANES:(q + 1) * LANES] for i in range(8)], axis=0
            )
            send[h, q * 16:(q + 1) * 16] = rows.T.reshape(16, PB, LANES)

    speeds = cour_ref[...]
    lane = lax.broadcasted_iota(jnp.int32, (8, LANES), 1)
    even = jnp.zeros((8, LANES), F32)
    odd = jnp.zeros((8, LANES), F32)
    for i in range(4):
        for is_odd in range(2):
            target = (is_odd * 4 + i) * GROUP
            shifts = [(target - i * 32 - cc * GROUP) % LANES for cc in range(2)]
            rolled = [pltpu.roll(speeds, s, 1) if s else speeds for s in shifts]
            here = (lane // GROUP) == (is_odd * 4 + i)
            piece = jnp.where(core == 0, rolled[0], rolled[1])
            if is_odd:
                odd = jnp.where(here, piece, odd)
            else:
                even = jnp.where(here, piece, even)
    for t in range(4):
        row = jnp.where(lane < 64, even[2 * t:2 * t + 1], odd[2 * t + 1:2 * t + 2])
        cour[t] = row

    pl.semaphore_wait(barrier, len(OFFSETS) + 3)

    rate_copy = pltpu.make_async_remote_copy(
        rate_ref, rates.at[z_lo], rate_sem.at[0], rate_sem.at[1], device_id=level, device_id_type=MESH
    )
    for phase in range(2):
        h = z_lo if phase == 0 else 1 - z_lo
        for o in OFFSETS:
            xx, zz = far(o)
            pltpu.make_async_remote_copy(
                send.at[h, xx * RING + zz], recv.at[phase, z_lo, z_hi, x],
                a2a_ss.at[phase], a2a_rs.at[phase],
                device_id=device(xx, y, zz, core), device_id_type=MESH,
            ).start()
        pltpu.make_async_copy(
            send.at[h, block], recv.at[phase, z_lo, z_hi, x], a2a_rs.at[phase]
        ).start()
        if phase == 0:
            rate_copy.start()

    m_at = lax.broadcasted_iota(jnp.int32, (256, 256), 0)
    n_at = lax.broadcasted_iota(jnp.int32, (256, 256), 1)
    whose = jnp.where(m_at < LANES, core, 1 - core)
    inner = m_at % LANES
    pick = (n_at == (inner // GROUP) * 32 + whose * GROUP + inner % GROUP).astype(F32).astype(BF16)
    for k in range(2):
        mats[k].wait()
        for b in range(4):
            block_cols = raw[k, :, :, b * 256:(b + 1) * 256].reshape(HALF, 256)
            res = lax.dot_general(
                pick, block_cols, (((1,), (1,)), ((), ())), preferred_element_type=F32
            ).astype(BF16)
            turned[k, b * LANES:(b + 1) * LANES] = res[:LANES]
            turned[k, HALF + b * LANES:HALF + (b + 1) * LANES] = res[LANES:]

    rates[z_lo] = rate_ref[...]
    rate_copy.wait()
    rate_cols[...] = jnp.zeros_like(rate_cols)
    cell_tile = pl.multiple_of((block // 16) * LANES, LANES)
    rate_cols[0:16] = rates[0, :, pl.ds(cell_tile, LANES)]
    rate_cols[16:32] = rates[1, :, pl.ds(cell_tile, LANES)]
    rate_cols[...] = rate_cols[...].T
    column = rate_cols[pl.ds(pl.multiple_of((block % 16) * PB, PB), PB), :]
    for i in range(SLAB):
        rate_b[i] = jnp.broadcast_to(column[:, i:i + 1], (PB, LANES))

    def arrived(phase):
        pltpu.make_async_copy(recv.at[phase], recv.at[phase], a2a_rs.at[phase]).wait()

    def unpack(phase):
        for zl in range(2):
            h = zl if phase == 0 else 1 - zl
            for t in range(4):
                tiles = swap_groups([recv[phase, zl, t, g] for g in range(8)])
                for i in range(8):
                    state[zl * 16 + h * 8 + i, :, t * LANES:(t + 1) * LANES] = tiles[i]

    def halo_copies(step):
        return [
            pltpu.make_async_remote_copy(
                state.at[pl.ds(SLAB - HALO, HALO)], halo.at[step, 0], halo_ss.at[step, 0],
                halo_rs.at[step, 0], device_id=up_dev, device_id_type=MESH,
            ),
            pltpu.make_async_remote_copy(
                state.at[pl.ds(0, HALO)], halo.at[step, 1], halo_ss.at[step, 1],
                halo_rs.at[step, 1], device_id=down_dev, device_id_type=MESH,
            ),
        ]

    arrived(0)
    unpack(0)
    halos = halo_copies(0)
    for c in halos:
        c.start()
    arrived(1)
    unpack(1)

    for step in range(STEPS):
        for c in halos:
            c.wait()
        for t in range(4):
            cols = slice(t * LANES, (t + 1) * LANES)
            c = cour[t]
            up, down = jnp.maximum(c, 0.0), jnp.minimum(c, 0.0)
            ahead, behind = 0.5 * (1.0 - c), 0.5 * (1.0 + c)
            for lo in range(0, SLAB, 16):
                planes = []
                for i in range(lo - HALO, lo + 16 + HALO):
                    if i < 0:
                        planes.append(halo[step, 0, i + HALO, :, cols])
                    elif i >= SLAB:
                        planes.append(halo[step, 1, i - SLAB, :, cols])
                    else:
                        planes.append(state[i, :, cols])
                less = sweep(planes, up, down, ahead, behind)
                section = [planes[i] - less[i] for i in range(2, len(planes) - 2)]
                less2 = sweep(section, up, down, ahead, behind)
                result = [
                    0.5 * planes[i + 2] + 0.5 * (section[i] - less2[i])
                    for i in range(2, len(section) - 2)
                ]
                for i in range(0, 16, 2):
                    smooth[lo + i, :, cols] = result[i]
                    smooth[lo + i + 1, :, cols] = result[i + 1]
                    pair = jnp.concatenate([result[i], result[i + 1]], axis=0)
                    ownr[step, (lo + i) * PB:(lo + i + 2) * PB, cols] = pair.astype(BF16)
        share = pltpu.make_async_remote_copy(
            ownr.at[step], parr.at[step], core_ss.at[step], core_rs.at[step],
            device_id=twin, device_id_type=MESH,
        )
        share.start()
        first[...] = jnp.dot(ownr[step], turned[0, :HALF], preferred_element_type=F32)
        second[...] = jnp.dot(ownr[step], turned[1, :HALF], preferred_element_type=F32)
        share.wait()
        first[...] += jnp.dot(parr[step], turned[0, HALF:], preferred_element_type=F32)
        second[...] += jnp.dot(parr[step], turned[1, HALF:], preferred_element_type=F32)
        for i in range(0, SLAB, 2):
            rows = slice(i * PB, (i + 2) * PB)
            gained = (first[rows] * second[rows]).astype(BF16).astype(F32)
            rounded = ownr[step, rows].astype(F32)
            for j in range(2):
                part = slice(j * PB, (j + 1) * PB)
                rate = jnp.concatenate([rate_b[i + j]] * 4, axis=1)
                state[i + j] = smooth[i + j] + TIME_STEP * (gained[part] - rate * rounded[part])
        if step + 1 < STEPS:
            halos = halo_copies(step + 1)
            for c in halos:
                c.start()

    for zl in range(2):
        for h in range(2):
            for t in range(4):
                tiles = swap_groups(
                    [state[zl * 16 + h * 8 + i, :, t * LANES:(t + 1) * LANES] for i in range(8)]
                )
                for g in range(8):
                    sout[h, g, t * 2 + zl] = tiles[g]
    for h in range(2):
        for o in OFFSETS:
            xx, zz = far(o)
            pltpu.make_async_remote_copy(
                sout.at[h, xx, zz], outr.at[h, block], out_ss.at[h], out_rs.at[h],
                device_id=device(xx, y, zz, core), device_id_type=MESH,
            ).start()
        pltpu.make_async_copy(sout.at[h, x, z], outr.at[h, block], out_rs.at[h]).start()
    for h in range(2):
        pltpu.make_async_copy(outr.at[h], outr.at[h], out_rs.at[h]).wait()
        for q in range(4):
            rows = outr[h, q * 16:(q + 1) * 16].reshape(LANES, LANES).T
            out_ref[h * 8:(h + 1) * 8, :, q * LANES:(q + 1) * LANES] = rows.reshape(8, 16, LANES)
    for phase in range(2):
        sent = send.at[0, pl.ds(0, len(OFFSETS))]
        pltpu.make_async_copy(sent, sent, a2a_ss.at[phase]).wait()
        pltpu.make_async_copy(sent, sent, out_ss.at[phase]).wait()


def body(distribution, courant, gain_matrix, product_matrix, collision_rate):
    dma = pltpu.SemaphoreType.DMA
    planes = pl.pallas_call(
        kernel,
        out_shape=jax.ShapeDtypeStruct((16, GROUP, 512), F32),
        in_specs=[
            pl.BlockSpec(memory_space=pl.ANY),
            pl.BlockSpec(memory_space=pltpu.VMEM),
            pl.BlockSpec(memory_space=pl.ANY),
            pl.BlockSpec(memory_space=pl.ANY),
            pl.BlockSpec(memory_space=pltpu.VMEM),
        ],
        out_specs=pl.BlockSpec(memory_space=pltpu.VMEM),
        scratch_shapes=[
            pltpu.VMEM((GROUP, 16, 512), F32),
            pltpu.VMEM((2, 64, PB, LANES), F32),
            pltpu.VMEM((2, 2, 4, 8, PB, LANES), F32),
            pltpu.VMEM((SLAB, PB, HALF), F32),
            pltpu.VMEM((SLAB, PB, HALF), F32),
            pltpu.VMEM((STEPS, SLAB * PB, HALF), BF16),
            pltpu.VMEM((STEPS, SLAB * PB, HALF), BF16),
            pltpu.VMEM((STEPS, 2, HALO, PB, HALF), F32),
            pltpu.VMEM((2, 32, GROUP, 1024), BF16),
            pltpu.VMEM((2, 1024, HALF), BF16),
            pltpu.VMEM((SLAB * PB, HALF), F32),
            pltpu.VMEM((SLAB * PB, HALF), F32),
            pltpu.VMEM((4, 8, LANES), F32),
            pltpu.VMEM((2, 16, 512), F32),
            pltpu.VMEM((LANES, LANES), F32),
            pltpu.VMEM((SLAB, PB, LANES), F32),
            pltpu.VMEM((2, 8, 8, PB, LANES), F32),
            pltpu.VMEM((2, 64, PB, LANES), F32),
            dma, dma((2,)), dma((2,)), dma((2,)), dma((STEPS, 2)), dma((STEPS, 2)),
            dma((STEPS,)), dma((STEPS,)), dma((2,)), dma((2,)), dma((2,)),
        ],
        compiler_params=pltpu.CompilerParams(collective_id=0, has_side_effects=True),
        name="boltzmann",
    )(
        distribution,
        courant.reshape(8, LANES),
        gain_matrix.reshape(32, 2, GROUP, 1024),
        product_matrix.reshape(32, 2, GROUP, 1024),
        collision_rate,
    )
    return jnp.transpose(planes, (1, 0, 2))


def solution(mesh):
    in_specs = (P("vel", "space", None), P(), P(), P(), P("space", None))
    out_specs = P("vel", "space", None)
    return jax.shard_map(body, mesh=mesh, in_specs=in_specs, out_specs=out_specs, check_vma=False)
```

```python
import functools

import jax
import jax.numpy as jnp
from jax import lax
from jax.experimental import pallas as pl
from jax.experimental.pallas import tpu as pltpu
from jax.sharding import PartitionSpec as P

STEPS = 2
TIME_STEP = 0.2
MESH = pl.DeviceIdType.MESH
F32 = jnp.float32
BF16 = jnp.bfloat16
RING = 8
LANES = 128
GROUP = 16
PB = 8
SLAB = 32
HALO = 4
SPAN = 2.0 ** 30
HALF = 512

OFFSETS = sorted(
    [(dx, dz) for dx in range(RING) for dz in range(RING) if (dx, dz) != (0, 0)],
    key=lambda o: -(min(o[0], RING - o[0]) + min(o[1], RING - o[1])),
)
BACK = sorted(
    [(j, dx) for j in range(4) for dx in range(RING)],
    key=lambda o: -(min(2 * o[0], RING - 2 * o[0]) + min(o[1], RING - o[1])),
)


def coords():
    vel, space = lax.axis_index("vel"), lax.axis_index("space")
    z_hi, x, core = vel // 16, (vel // 2) % 8, vel % 2
    y, z_lo = space // 2, space % 2
    return x, y, z_hi, z_lo, core


def device(x, y, z, core):
    return {"vel": (z // 2) * 16 + x * 2 + core, "space": y * 2 + z % 2}


def swap_groups(tiles):
    lane = lax.broadcasted_iota(jnp.int32, (8, LANES), 1) // GROUP
    tiles = list(tiles)
    for bit in (4, 2, 1):
        low = (lane & bit) == 0
        for i in range(8):
            if i & bit:
                continue
            j = i | bit
            a, b = tiles[i], tiles[j]
            tiles[i] = jnp.where(low, a, pltpu.roll(b, bit * GROUP, 1))
            tiles[j] = jnp.where(low, pltpu.roll(a, LANES - bit * GROUP, 1), b)
    return tiles


def encode(values):
    square = values * values
    power = square * square
    return jnp.where(values < 0.0, -power, power)


def decode(powers):
    root = jnp.sqrt(jnp.sqrt(jnp.abs(powers)))
    return jnp.where(powers < 0.0, -root, root)


def minmod(a, b):
    return jnp.maximum(jnp.minimum(a, b), 0.0) + jnp.minimum(jnp.maximum(a, b), 0.0)


def sweep(values, up, down, ahead, behind):
    n = len(values)
    differ = [values[i + 1] - values[i] for i in range(n - 1)]
    slopes = [None] + [minmod(differ[i], differ[i - 1]) for i in range(1, n - 1)]
    fluxes = {}
    for i in range(1, n - 2):
        fluxes[i] = up * (values[i] + ahead * slopes[i]) + down * (
            values[i + 1] - behind * slopes[i + 1]
        )
    return {i: fluxes[i] - fluxes[i - 1] for i in range(2, n - 2)}


def kernel(
    dist_ref, cour_ref, gain_ref, prod_ref, rate_ref, out_ref, unit_ref,
    sin, send, recv, state, later, smooth, ownr, parr, halo, raw, turned, first, second,
    cour, rates, rate_cols, rate_b, sout, sunit,
    in_sem, mat_sem, a2a_ss, a2a_rs, halo_ss, halo_rs, core_ss, core_rs,
    rate_sem, out_ss, out_rs, unit_ss, unit_rs,
):
    x, y, z_hi, z_lo, core = coords()
    z = z_hi * 2 + z_lo
    block = x * RING + z
    up_dev = device(x, lax.rem(y + 1, RING), z, core)
    down_dev = device(x, lax.rem(y + RING - 1, RING), z, core)
    twin = device(x, y, z, 1 - core)
    level = device(x, y, z_hi * 2 + 1 - z_lo, core)

    turn = 1 - 2 * core

    def far(o):
        return lax.rem(x + RING + turn * o[0], RING), lax.rem(z + RING + turn * o[1], RING)

    barrier = pltpu.get_barrier_semaphore()
    for o in OFFSETS:
        xx, zz = far(o)
        pl.semaphore_signal(barrier, 1, device_id=device(xx, y, zz, core), device_id_type=MESH)
    for peer in (up_dev, down_dev, twin):
        pl.semaphore_signal(barrier, 1, device_id=peer, device_id_type=MESH)

    load = pltpu.make_async_copy(dist_ref, sin, in_sem)
    load.start()
    mats = [
        pltpu.make_async_copy(gain_ref.at[:, core], raw.at[0], mat_sem.at[0]),
        pltpu.make_async_copy(prod_ref.at[:, core], raw.at[1], mat_sem.at[1]),
    ]
    for m in mats:
        m.start()
    load.wait()

    for h in range(2):
        for q in range(4):
            rows = jnp.concatenate(
                [sin[:, h * 8 + i, q * LANES:(q + 1) * LANES] for i in range(8)], axis=0
            )
            send[h, q * 16:(q + 1) * 16] = rows.T.reshape(16, PB, LANES)

    pl.semaphore_wait(barrier, len(OFFSETS) + 3)

    rate_copy = pltpu.make_async_remote_copy(
        rate_ref, rates.at[z_lo], rate_sem.at[0], rate_sem.at[1], device_id=level, device_id_type=MESH
    )
    def send_phase(phase):
        h = z_lo if phase == 0 else 1 - z_lo
        for o in OFFSETS:
            xx, zz = far(o)
            pltpu.make_async_remote_copy(
                send.at[h, xx * RING + zz], recv.at[phase, z_lo, z_hi, x],
                a2a_ss.at[phase], a2a_rs.at[phase],
                device_id=device(xx, y, zz, core), device_id_type=MESH,
            ).start()
        pltpu.make_async_copy(
            send.at[h, block], recv.at[phase, z_lo, z_hi, x], a2a_rs.at[phase]
        ).start()

    rate_copy.start()
    send_phase(0)

    speeds = cour_ref[...]
    lane = lax.broadcasted_iota(jnp.int32, (8, LANES), 1)
    even = jnp.zeros((8, LANES), F32)
    odd = jnp.zeros((8, LANES), F32)
    for i in range(4):
        for is_odd in range(2):
            target = (is_odd * 4 + i) * GROUP
            shifts = [(target - i * 32 - cc * GROUP) % LANES for cc in range(2)]
            rolled = [pltpu.roll(speeds, s, 1) if s else speeds for s in shifts]
            here = (lane // GROUP) == (is_odd * 4 + i)
            piece = jnp.where(core == 0, rolled[0], rolled[1])
            if is_odd:
                odd = jnp.where(here, piece, odd)
            else:
                even = jnp.where(here, piece, even)
    for t in range(4):
        cour[t] = jnp.where(lane < 64, even[2 * t:2 * t + 1], odd[2 * t + 1:2 * t + 2])

    m_at = lax.broadcasted_iota(jnp.int32, (256, 256), 0)
    n_at = lax.broadcasted_iota(jnp.int32, (256, 256), 1)
    whose = jnp.where(m_at < LANES, core, 1 - core)
    inner = m_at % LANES
    pick = (n_at == (inner // GROUP) * 32 + whose * GROUP + inner % GROUP).astype(F32).astype(BF16)
    for k in range(2):
        mats[k].wait()
        for b in range(4):
            block_cols = raw[k, :, :, b * 256:(b + 1) * 256].reshape(HALF, 256)
            res = lax.dot_general(
                pick, block_cols, (((1,), (1,)), ((), ())), preferred_element_type=F32
            ).astype(BF16)
            turned[k, b * LANES:(b + 1) * LANES] = res[:LANES]
            turned[k, HALF + b * LANES:HALF + (b + 1) * LANES] = res[LANES:]

    def spread_rates():
        rates[z_lo] = rate_ref[...]
        rate_copy.wait()
        rate_cols[...] = jnp.zeros_like(rate_cols)
        cell_tile = pl.multiple_of((block // 16) * LANES, LANES)
        rate_cols[0:16] = rates[0, :, pl.ds(cell_tile, LANES)]
        rate_cols[16:32] = rates[1, :, pl.ds(cell_tile, LANES)]
        rate_cols[...] = rate_cols[...].T
        column = rate_cols[pl.ds(pl.multiple_of((block % 16) * PB, PB), PB), :]
        for i in range(SLAB):
            rate_b[i] = jnp.broadcast_to(column[:, i:i + 1], (PB, LANES))

    def arrived(phase):
        pltpu.make_async_copy(recv.at[phase], recv.at[phase], a2a_rs.at[phase]).wait()

    def unpack(phase):
        for zl in range(2):
            h = zl if phase == 0 else 1 - zl
            for t in range(4):
                tiles = swap_groups([recv[phase, zl, t, g] for g in range(8)])
                for i in range(8):
                    state[zl * 16 + h * 8 + i, :, t * LANES:(t + 1) * LANES] = tiles[i]

    def send_faces(source, step):
        copies = [
            pltpu.make_async_remote_copy(
                source.at[pl.ds(SLAB - HALO, HALO)], halo.at[step, 0], halo_ss.at[step, 0],
                halo_rs.at[step, 0], device_id=up_dev, device_id_type=MESH,
            ),
            pltpu.make_async_remote_copy(
                source.at[pl.ds(0, HALO)], halo.at[step, 1], halo_ss.at[step, 1],
                halo_rs.at[step, 1], device_id=down_dev, device_id_type=MESH,
            ),
        ]
        for c in copies:
            c.start()
        return copies

    def advect(source, step, lo, count):
        for t in range(4):
            cols = slice(t * LANES, (t + 1) * LANES)
            c = cour[t]
            up, down = jnp.maximum(c, 0.0), jnp.minimum(c, 0.0)
            ahead, behind = 0.5 * (1.0 - c), 0.5 * (1.0 + c)
            planes = []
            for i in range(lo - HALO, lo + count + HALO):
                if i < 0:
                    planes.append(halo[step, 0, i + HALO, :, cols])
                elif i >= SLAB:
                    planes.append(halo[step, 1, i - SLAB, :, cols])
                else:
                    planes.append(source[i, :, cols])
            less = sweep(planes, up, down, ahead, behind)
            section = [planes[i] - less[i] for i in range(2, len(planes) - 2)]
            less2 = sweep(section, up, down, ahead, behind)
            result = [
                0.5 * planes[i + 2] + 0.5 * (section[i] - less2[i])
                for i in range(2, len(section) - 2)
            ]
            for i in range(0, count, 2):
                smooth[lo + i, :, cols] = result[i]
                smooth[lo + i + 1, :, cols] = result[i + 1]
                pair = jnp.concatenate([result[i], result[i + 1]], axis=0)
                ownr[step, (lo + i) * PB:(lo + i + 2) * PB, cols] = pair.astype(BF16)

    def share(step, number, lo, count):
        rows = pl.ds(lo * PB, count * PB)
        copy = pltpu.make_async_remote_copy(
            ownr.at[step, rows], parr.at[step, rows], core_ss.at[number], core_rs.at[number],
            device_id=twin, device_id_type=MESH,
        )
        copy.start()
        return copy

    def rows_of(ref, step, ranges):
        parts = [ref[step, lo * PB:(lo + count) * PB] for lo, count in ranges]
        return parts[0] if len(parts) == 1 else jnp.concatenate(parts, axis=0)

    def products(source, step, ranges, half, add):
        block_rows = rows_of(source, step, ranges)
        for k, total in ((0, first), (1, second)):
            value = jnp.dot(
                block_rows, turned[k, half * HALF:(half + 1) * HALF], preferred_element_type=F32
            )
            at = 0
            for lo, count in ranges:
                rows = slice(lo * PB, (lo + count) * PB)
                part = value[at:at + count * PB]
                total[rows] = total[rows] + part if add else part
                at += count * PB

    def update(target, step, ranges):
        for lo, count in ranges:
            for i in range(lo, lo + count, 2):
                rows = slice(i * PB, (i + 2) * PB)
                gained = (first[rows] * second[rows]).astype(BF16).astype(F32)
                rounded = ownr[step, rows].astype(F32)
                for j in range(2):
                    part = slice(j * PB, (j + 1) * PB)
                    rate = jnp.concatenate([rate_b[i + j]] * 4, axis=1)
                    target[i + j] = smooth[i + j] + TIME_STEP * (
                        gained[part] - rate * rounded[part]
                    )

    arrived(0)
    send_phase(1)
    unpack(0)
    faces = send_faces(state, 0)
    spread_rates()
    for c in faces:
        c.wait()
    edges = ((0, HALO), (SLAB - HALO, HALO))
    shares = []
    for n, (lo, count) in enumerate(edges):
        advect(state, 0, lo, count)
        shares.append(share(0, n, lo, count))
    products(ownr, 0, edges, 0, False)
    for c in shares:
        c.wait()
    products(parr, 0, edges, 1, True)
    update(later, 0, edges)
    faces = send_faces(later, 1)
    arrived(1)
    unpack(1)
    inside = ((HALO, 12), (HALO + 12, 12))
    shares = []
    for n, (lo, count) in enumerate(inside):
        advect(state, 0, lo, count)
        shares.append(share(0, 2 + n, lo, count))
    inside = ((HALO, 24),)
    products(ownr, 0, inside, 0, False)
    for c in shares:
        c.wait()
    products(parr, 0, inside, 1, True)
    update(later, 0, inside)
    for c in faces:
        c.wait()

    def dispatch(zl):
        odd = lax.rem(z_lo + zl, 2)
        for j, dx in BACK:
            xx, zz = far((dx, 2 * j + odd))
            t = zz // 2

            def remote():
                to = device(xx, y, zz, core)
                pltpu.make_async_remote_copy(
                    sunit.at[zl], unit_ref.at[block], unit_ss, unit_rs,
                    device_id=to, device_id_type=MESH,
                ).start()
                pltpu.make_async_remote_copy(
                    sout.at[zl, xx, t], out_ref.at[block], out_ss, out_rs,
                    device_id=to, device_id_type=MESH,
                ).start()

            if j or dx:
                remote()
            else:
                pl.when(odd == 1)(remote)

                @pl.when(odd == 0)
                def _():
                    pltpu.make_async_copy(sunit.at[zl], unit_ref.at[block], unit_rs).start()
                    pltpu.make_async_copy(sout.at[zl, x, t], out_ref.at[block], out_rs).start()

    shares = []
    for zl in range(2):
        advect(later, 1, zl * 16, 16)
        shares.append(share(1, 4 + zl, zl * 16, 16))
    for zl in range(2):
        part = ((zl * 16, 16),)
        products(ownr, 1, part, 0, False)
        shares[zl].wait()
        products(parr, 1, part, 1, True)
        update(state, 1, part)
        top = jnp.abs(state[zl * 16])
        for i in range(1, 16):
            top = jnp.maximum(top, jnp.abs(state[zl * 16 + i]))
        top = jnp.maximum(jnp.max(top, axis=(0, 1), keepdims=True), 1e-20)
        unit = jnp.broadcast_to(top * (1.0 / SPAN), (PB, LANES)).astype(BF16).astype(F32)
        sunit[zl] = unit[:1]
        scale = 1.0 / unit
        for t in range(4):
            pair = [
                swap_groups(
                    [
                        encode(state[zl * 16 + h * 8 + i, :, t * LANES:(t + 1) * LANES] * scale)
                        for i in range(8)
                    ]
                )
                for h in range(2)
            ]
            for g in range(8):
                sout[zl, g, t] = jnp.concatenate([pair[0][g], pair[1][g]], axis=0).astype(BF16)
        dispatch(zl)

    pltpu.make_async_copy(out_ref, out_ref, out_rs).wait()
    pltpu.make_async_copy(unit_ref, unit_ref, unit_rs).wait()
    sent = out_ref.at[pl.ds(0, len(OFFSETS))]
    pltpu.make_async_copy(sent, sent, out_ss).wait()
    sent = unit_ref.at[pl.ds(0, len(OFFSETS))]
    pltpu.make_async_copy(sent, sent, unit_ss).wait()
    for phase in range(2):
        sent = send.at[0, pl.ds(0, len(OFFSETS))]
        pltpu.make_async_copy(sent, sent, a2a_ss.at[phase]).wait()


def place(tiles_ref, unit_ref, out_ref):
    m_at = lax.broadcasted_iota(jnp.int32, (LANES, LANES), 0)
    n_at = lax.broadcasted_iota(jnp.int32, (LANES, LANES), 1)
    order = (n_at == (m_at % 8) * GROUP + m_at // 8).astype(F32).astype(BF16)
    last = (((1,), (1,)), ((), ()))
    for q in range(4):
        part = slice(q * 16, (q + 1) * 16)
        cols = slice(q * LANES, (q + 1) * LANES)
        units = jnp.broadcast_to(unit_ref[part], (16, PB, LANES)).reshape(LANES, LANES).astype(BF16)
        unit = lax.dot_general(order[:8], units, last, preferred_element_type=F32)
        tiles = tiles_ref[part].astype(F32)
        for h in range(2):
            block = tiles[:, h * PB:(h + 1) * PB].reshape(LANES, LANES).astype(BF16)
            rows = lax.dot_general(order, block, last, preferred_element_type=F32)
            out_ref[:, h * 8:(h + 1) * 8, cols] = decode(rows).reshape(GROUP, 8, LANES) * unit


def body(distribution, courant, gain_matrix, product_matrix, collision_rate):
    dma = pltpu.SemaphoreType.DMA
    tiles, units = pl.pallas_call(
        kernel,
        out_shape=(
            jax.ShapeDtypeStruct((64, 2 * PB, LANES), BF16),
            jax.ShapeDtypeStruct((64, 1, LANES), F32),
        ),
        in_specs=[
            pl.BlockSpec(memory_space=pl.ANY),
            pl.BlockSpec(memory_space=pltpu.VMEM),
            pl.BlockSpec(memory_space=pl.ANY),
            pl.BlockSpec(memory_space=pl.ANY),
            pl.BlockSpec(memory_space=pltpu.VMEM),
        ],
        out_specs=(pl.BlockSpec(memory_space=pl.ANY), pl.BlockSpec(memory_space=pl.ANY)),
        scratch_shapes=[
            pltpu.VMEM((GROUP, 16, 512), F32),
            pltpu.VMEM((2, 64, PB, LANES), F32),
            pltpu.VMEM((2, 2, 4, 8, PB, LANES), F32),
            pltpu.VMEM((SLAB, PB, HALF), F32),
            pltpu.VMEM((SLAB, PB, HALF), F32),
            pltpu.VMEM((SLAB, PB, HALF), F32),
            pltpu.VMEM((STEPS, SLAB * PB, HALF), BF16),
            pltpu.VMEM((STEPS, SLAB * PB, HALF), BF16),
            pltpu.VMEM((STEPS, 2, HALO, PB, HALF), F32),
            pltpu.VMEM((2, 32, GROUP, 1024), BF16),
            pltpu.VMEM((2, 1024, HALF), BF16),
            pltpu.VMEM((SLAB * PB, HALF), F32),
            pltpu.VMEM((SLAB * PB, HALF), F32),
            pltpu.VMEM((4, 8, LANES), F32),
            pltpu.VMEM((2, 16, 512), F32),
            pltpu.VMEM((LANES, LANES), F32),
            pltpu.VMEM((SLAB, PB, LANES), F32),
            pltpu.VMEM((2, 8, 4, 2 * PB, LANES), BF16),
            pltpu.VMEM((2, 1, LANES), F32),
            dma, dma((2,)), dma((2,)), dma((2,)), dma((STEPS, 2)), dma((STEPS, 2)),
            dma((6,)), dma((6,)), dma((2,)), dma, dma, dma, dma,
        ],
        compiler_params=pltpu.CompilerParams(collective_id=0, has_side_effects=True),
        name="boltzmann",
    )(
        distribution,
        courant.reshape(8, LANES),
        gain_matrix.reshape(32, 2, GROUP, 1024),
        product_matrix.reshape(32, 2, GROUP, 1024),
        collision_rate,
    )
    return pl.pallas_call(
        place,
        out_shape=jax.ShapeDtypeStruct((GROUP, 16, 512), F32),
        in_specs=[pl.BlockSpec(memory_space=pltpu.VMEM)] * 2,
        out_specs=pl.BlockSpec(memory_space=pltpu.VMEM),
        name="place",
    )(tiles, units)


def solution(mesh):
    in_specs = (P("vel", "space", None), P(), P(), P(), P("space", None))
    out_specs = P("vel", "space", None)
    return jax.shard_map(body, mesh=mesh, in_specs=in_specs, out_specs=out_specs, check_vma=False)
```

```python
import functools

import jax
import jax.numpy as jnp
from jax import lax
from jax.experimental import pallas as pl
from jax.experimental.pallas import tpu as pltpu
from jax.sharding import PartitionSpec as P

STEPS = 2
TIME_STEP = 0.2
MESH = pl.DeviceIdType.MESH
F32 = jnp.float32
BF16 = jnp.bfloat16
RING = 8
LANES = 128
GROUP = 16
PB = 8
SLAB = 32
HALO = 4
SPAN = 2.0 ** 30
HALF = 512

OFFSETS = sorted(
    [(dx, dz) for dx in range(RING) for dz in range(RING) if (dx, dz) != (0, 0)],
    key=lambda o: -(min(o[0], RING - o[0]) + min(o[1], RING - o[1])),
)


def coords():
    vel, space = lax.axis_index("vel"), lax.axis_index("space")
    z_hi, x, core = vel // 16, (vel // 2) % 8, vel % 2
    y, z_lo = space // 2, space % 2
    return x, y, z_hi, z_lo, core


def device(x, y, z, core):
    return {"vel": (z // 2) * 16 + x * 2 + core, "space": y * 2 + z % 2}


def swap_groups(tiles):
    lane = lax.broadcasted_iota(jnp.int32, (8, LANES), 1) // GROUP
    tiles = list(tiles)
    for bit in (4, 2, 1):
        low = (lane & bit) == 0
        for i in range(8):
            if i & bit:
                continue
            j = i | bit
            a, b = tiles[i], tiles[j]
            tiles[i] = jnp.where(low, a, pltpu.roll(b, bit * GROUP, 1))
            tiles[j] = jnp.where(low, pltpu.roll(a, LANES - bit * GROUP, 1), b)
    return tiles


def encode(values):
    square = values * values
    power = square * square
    return jnp.where(values < 0.0, -power, power)


def decode(powers):
    root = jnp.sqrt(jnp.sqrt(jnp.abs(powers)))
    return jnp.where(powers < 0.0, -root, root)


def sweep(values, speed, rising, reach):
    n = len(values)
    differ = [values[i + 1] - values[i] for i in range(n - 1)]
    slopes = [None] + [
        jnp.maximum(
            jnp.minimum(differ[i], jnp.maximum(differ[i - 1], 0.0)),
            jnp.minimum(differ[i - 1], 0.0),
        )
        for i in range(1, n - 1)
    ]
    fluxes = {}
    for i in range(1, n - 2):
        value = jnp.where(rising, values[i], values[i + 1])
        slope = jnp.where(rising, slopes[i], slopes[i + 1])
        fluxes[i] = speed * (value + reach * slope)
    return {i: fluxes[i] - fluxes[i - 1] for i in range(2, n - 2)}


def kernel(
    dist_ref, cour_ref, gain_ref, prod_ref, rate_ref, out_ref, unit_ref,
    sin, send, recv, state, later, smooth, ownr, parr, halo, raw, turned, first, second,
    cour, rates, rate_cols, rate_b, sout, sunit,
    in_sem, mat_sem, a2a_ss, a2a_rs, halo_ss, halo_rs, core_ss, core_rs,
    rate_sem, out_ss, out_rs, unit_ss, unit_rs, gone,
):
    x, y, z_hi, z_lo, core = coords()
    z = z_hi * 2 + z_lo
    block = x * RING + z
    up_dev = device(x, lax.rem(y + 1, RING), z, core)
    down_dev = device(x, lax.rem(y + RING - 1, RING), z, core)
    twin = device(x, y, z, 1 - core)
    level = device(x, y, z_hi * 2 + 1 - z_lo, core)

    turn = 1 - 2 * core

    def far(o):
        return lax.rem(x + RING + turn * o[0], RING), lax.rem(z + RING + turn * o[1], RING)

    barrier = pltpu.get_barrier_semaphore()
    for o in OFFSETS:
        xx, zz = far(o)
        pl.semaphore_signal(barrier, 1, device_id=device(xx, y, zz, core), device_id_type=MESH)
    for peer in (up_dev, down_dev, twin):
        pl.semaphore_signal(barrier, 1, device_id=peer, device_id_type=MESH)

    load = pltpu.make_async_copy(dist_ref, sin, in_sem)
    load.start()
    mats = [
        pltpu.make_async_copy(gain_ref.at[:, core], raw.at[0], mat_sem.at[0]),
        pltpu.make_async_copy(prod_ref.at[:, core], raw.at[1], mat_sem.at[1]),
    ]
    for m in mats:
        m.start()
    load.wait()

    for h in range(2):
        for q in range(4):
            rows = jnp.concatenate(
                [sin[:, h * 8 + i, q * LANES:(q + 1) * LANES] for i in range(8)], axis=0
            )
            send[h, q * 16:(q + 1) * 16] = rows.T.reshape(16, PB, LANES)

    pl.semaphore_wait(barrier, len(OFFSETS) + 3)

    rate_copy = pltpu.make_async_remote_copy(
        rate_ref, rates.at[z_lo], rate_sem.at[0], rate_sem.at[1], device_id=level, device_id_type=MESH
    )
    def send_phase(phase):
        h = z_lo if phase == 0 else 1 - z_lo
        for o in OFFSETS:
            xx, zz = far(o)
            pltpu.make_async_remote_copy(
                send.at[h, xx * RING + zz], recv.at[phase, z_lo, z_hi, x],
                a2a_ss.at[phase], a2a_rs.at[phase],
                device_id=device(xx, y, zz, core), device_id_type=MESH,
            ).start()
        pltpu.make_async_copy(
            send.at[h, block], recv.at[phase, z_lo, z_hi, x], a2a_rs.at[phase]
        ).start()

    rate_copy.start()
    send_phase(0)

    speeds = cour_ref[...]
    lane = lax.broadcasted_iota(jnp.int32, (8, LANES), 1)
    even = jnp.zeros((8, LANES), F32)
    odd = jnp.zeros((8, LANES), F32)
    for i in range(4):
        for is_odd in range(2):
            target = (is_odd * 4 + i) * GROUP
            shifts = [(target - i * 32 - cc * GROUP) % LANES for cc in range(2)]
            rolled = [pltpu.roll(speeds, s, 1) if s else speeds for s in shifts]
            here = (lane // GROUP) == (is_odd * 4 + i)
            piece = jnp.where(core == 0, rolled[0], rolled[1])
            if is_odd:
                odd = jnp.where(here, piece, odd)
            else:
                even = jnp.where(here, piece, even)
    for t in range(4):
        cour[t] = jnp.where(lane < 64, even[2 * t:2 * t + 1], odd[2 * t + 1:2 * t + 2])

    m_at = lax.broadcasted_iota(jnp.int32, (256, 256), 0)
    n_at = lax.broadcasted_iota(jnp.int32, (256, 256), 1)
    whose = jnp.where(m_at < LANES, core, 1 - core)
    inner = m_at % LANES
    pick = (n_at == (inner // GROUP) * 32 + whose * GROUP + inner % GROUP).astype(F32).astype(BF16)
    for k in range(2):
        mats[k].wait()
        for b in range(4):
            block_cols = raw[k, :, :, b * 256:(b + 1) * 256].reshape(HALF, 256)
            res = lax.dot_general(
                pick, block_cols, (((1,), (1,)), ((), ())), preferred_element_type=F32
            ).astype(BF16)
            turned[k, b * LANES:(b + 1) * LANES] = res[:LANES]
            turned[k, HALF + b * LANES:HALF + (b + 1) * LANES] = res[LANES:]

    def spread_rates():
        rates[z_lo] = rate_ref[...]
        rate_copy.wait()
        rate_cols[...] = jnp.zeros_like(rate_cols)
        cell_tile = pl.multiple_of((block // 16) * LANES, LANES)
        rate_cols[0:16] = rates[0, :, pl.ds(cell_tile, LANES)]
        rate_cols[16:32] = rates[1, :, pl.ds(cell_tile, LANES)]
        rate_cols[...] = rate_cols[...].T
        column = rate_cols[pl.ds(pl.multiple_of((block % 16) * PB, PB), PB), :]
        for i in range(SLAB):
            rate_b[i] = jnp.broadcast_to(column[:, i:i + 1], (PB, LANES))

    sent = send.at[0, pl.ds(0, len(OFFSETS))]
    pltpu.make_async_copy(sent, sent, a2a_ss.at[0]).wait()
    pl.semaphore_signal(gone, 1, device_id=twin, device_id_type=MESH)
    pl.semaphore_wait(gone, 1)
    send_phase(1)

    def arrived(phase):
        pltpu.make_async_copy(recv.at[phase], recv.at[phase], a2a_rs.at[phase]).wait()

    def unpack(phase):
        for zl in range(2):
            h = zl if phase == 0 else 1 - zl
            for t in range(4):
                tiles = swap_groups([recv[phase, zl, t, g] for g in range(8)])
                for i in range(8):
                    state[zl * 16 + h * 8 + i, :, t * LANES:(t + 1) * LANES] = tiles[i]

    def send_faces(source, step):
        copies = [
            pltpu.make_async_remote_copy(
                source.at[pl.ds(SLAB - HALO, HALO)], halo.at[step, 0], halo_ss.at[step, 0],
                halo_rs.at[step, 0], device_id=up_dev, device_id_type=MESH,
            ),
            pltpu.make_async_remote_copy(
                source.at[pl.ds(0, HALO)], halo.at[step, 1], halo_ss.at[step, 1],
                halo_rs.at[step, 1], device_id=down_dev, device_id_type=MESH,
            ),
        ]
        for c in copies:
            c.start()
        return copies

    def advect(source, step, lo, count):
        for t in range(4):
            cols = slice(t * LANES, (t + 1) * LANES)
            c = cour[t]
            rising = c > 0.0
            reach = jnp.where(rising, 0.5 * (1.0 - c), -(0.5 * (1.0 + c)))
            planes = []
            for i in range(lo - HALO, lo + count + HALO):
                if i < 0:
                    planes.append(halo[step, 0, i + HALO, :, cols])
                elif i >= SLAB:
                    planes.append(halo[step, 1, i - SLAB, :, cols])
                else:
                    planes.append(source[i, :, cols])
            less = sweep(planes, c, rising, reach)
            section = [planes[i] - less[i] for i in range(2, len(planes) - 2)]
            less2 = sweep(section, c, rising, reach)
            result = [
                0.5 * planes[i + 2] + 0.5 * (section[i] - less2[i])
                for i in range(2, len(section) - 2)
            ]
            for i in range(0, count, 2):
                smooth[lo + i, :, cols] = result[i]
                smooth[lo + i + 1, :, cols] = result[i + 1]
                pair = jnp.concatenate([result[i], result[i + 1]], axis=0)
                ownr[step, (lo + i) * PB:(lo + i + 2) * PB, cols] = pair.astype(BF16)

    def share(step, number, lo, count):
        rows = pl.ds(lo * PB, count * PB)
        copy = pltpu.make_async_remote_copy(
            ownr.at[step, rows], parr.at[step, rows], core_ss.at[number], core_rs.at[number],
            device_id=twin, device_id_type=MESH,
        )
        copy.start()
        return copy

    def rows_of(ref, step, ranges):
        parts = [ref[step, lo * PB:(lo + count) * PB] for lo, count in ranges]
        return parts[0] if len(parts) == 1 else jnp.concatenate(parts, axis=0)

    def products(source, step, ranges, half, add):
        block_rows = rows_of(source, step, ranges)
        for k, total in ((0, first), (1, second)):
            value = jnp.dot(
                block_rows, turned[k, half * HALF:(half + 1) * HALF], preferred_element_type=F32
            )
            at = 0
            for lo, count in ranges:
                rows = slice(lo * PB, (lo + count) * PB)
                part = value[at:at + count * PB]
                total[rows] = total[rows] + part if add else part
                at += count * PB

    def update(target, step, ranges):
        for lo, count in ranges:
            for i in range(lo, lo + count, 2):
                rows = slice(i * PB, (i + 2) * PB)
                gained = (first[rows] * second[rows]).astype(BF16).astype(F32)
                rounded = ownr[step, rows].astype(F32)
                for j in range(2):
                    part = slice(j * PB, (j + 1) * PB)
                    rate = jnp.concatenate([rate_b[i + j]] * 4, axis=1)
                    target[i + j] = smooth[i + j] + TIME_STEP * (
                        gained[part] - rate * rounded[part]
                    )

    arrived(0)
    unpack(0)
    faces = send_faces(state, 0)
    spread_rates()
    for c in faces:
        c.wait()
    edges = ((0, HALO), (SLAB - HALO, HALO))
    shares = []
    for n, (lo, count) in enumerate(edges):
        advect(state, 0, lo, count)
        shares.append(share(0, n, lo, count))
    products(ownr, 0, edges, 0, False)
    for c in shares:
        c.wait()
    products(parr, 0, edges, 1, True)
    update(later, 0, edges)
    faces = send_faces(later, 1)
    arrived(1)
    unpack(1)
    inside = ((HALO, 12), (HALO + 12, 12))
    shares = []
    for n, (lo, count) in enumerate(inside):
        advect(state, 0, lo, count)
        shares.append(share(0, 2 + n, lo, count))
    inside = ((HALO, 24),)
    products(ownr, 0, inside, 0, False)
    for c in shares:
        c.wait()
    products(parr, 0, inside, 1, True)
    update(later, 0, inside)
    for c in faces:
        c.wait()

    def dispatch(z_to):
        t, zl = z_to // 2, z_to % 2
        for dx in (4, 3, 5, 2, 6, 1, 7, 0):
            xx = lax.rem(x + RING + turn * dx, RING)

            def remote():
                to = device(xx, y, z_to, core)
                pltpu.make_async_remote_copy(
                    sunit.at[zl], unit_ref.at[block], unit_ss, unit_rs,
                    device_id=to, device_id_type=MESH,
                ).start()
                pltpu.make_async_remote_copy(
                    sout.at[zl, xx, t], out_ref.at[block], out_ss, out_rs,
                    device_id=to, device_id_type=MESH,
                ).start()

            if dx:
                remote()
            else:
                pl.when(z != z_to)(remote)

                @pl.when(z == z_to)
                def _():
                    pltpu.make_async_copy(sunit.at[zl], unit_ref.at[block], unit_rs).start()
                    pltpu.make_async_copy(sout.at[zl, x, t], out_ref.at[block], out_rs).start()

    shares = []
    for zl in range(2):
        advect(later, 1, zl * 16, 16)
        shares.append(share(1, 4 + zl, zl * 16, 16))
    for zl in range(2):
        part = ((zl * 16, 16),)
        products(ownr, 1, part, 0, False)
        shares[zl].wait()
        products(parr, 1, part, 1, True)
        update(state, 1, part)
        top = jnp.abs(state[zl * 16])
        for i in range(1, 16):
            top = jnp.maximum(top, jnp.abs(state[zl * 16 + i]))
        top = jnp.maximum(jnp.max(top, axis=(0, 1), keepdims=True), 1e-20)
        unit = jnp.broadcast_to(top * (1.0 / SPAN), (PB, LANES)).astype(BF16).astype(F32)
        sunit[zl] = unit[:1]
        scale = 1.0 / unit
        for t in range(4):
            pair = [
                swap_groups(
                    [
                        encode(state[zl * 16 + h * 8 + i, :, t * LANES:(t + 1) * LANES] * scale)
                        for i in range(8)
                    ]
                )
                for h in range(2)
            ]
            for g in range(8):
                sout[zl, g, t] = jnp.concatenate([pair[0][g], pair[1][g]], axis=0).astype(BF16)
        for z_to in (zl, zl + 2):
            dispatch(z_to)
    for z_to in (4, 5, 6, 7):
        dispatch(z_to)

    pltpu.make_async_copy(out_ref, out_ref, out_rs).wait()
    pltpu.make_async_copy(unit_ref, unit_ref, unit_rs).wait()
    sent = out_ref.at[pl.ds(0, len(OFFSETS))]
    pltpu.make_async_copy(sent, sent, out_ss).wait()
    sent = unit_ref.at[pl.ds(0, len(OFFSETS))]
    pltpu.make_async_copy(sent, sent, unit_ss).wait()
    sent = send.at[0, pl.ds(0, len(OFFSETS))]
    pltpu.make_async_copy(sent, sent, a2a_ss.at[1]).wait()


def place(tiles_ref, unit_ref, out_ref):
    m_at = lax.broadcasted_iota(jnp.int32, (LANES, LANES), 0)
    n_at = lax.broadcasted_iota(jnp.int32, (LANES, LANES), 1)
    order = (n_at == (m_at % 8) * GROUP + m_at // 8).astype(F32).astype(BF16)
    last = (((1,), (1,)), ((), ()))
    for q in range(4):
        part = slice(q * 16, (q + 1) * 16)
        cols = slice(q * LANES, (q + 1) * LANES)
        units = jnp.broadcast_to(unit_ref[part], (16, PB, LANES)).reshape(LANES, LANES).astype(BF16)
        unit = lax.dot_general(order[:8], units, last, preferred_element_type=F32)
        tiles = tiles_ref[part].astype(F32)
        for h in range(2):
            block = tiles[:, h * PB:(h + 1) * PB].reshape(LANES, LANES).astype(BF16)
            rows = lax.dot_general(order, block, last, preferred_element_type=F32)
            out_ref[:, h * 8:(h + 1) * 8, cols] = decode(rows).reshape(GROUP, 8, LANES) * unit


def body(distribution, courant, gain_matrix, product_matrix, collision_rate):
    dma = pltpu.SemaphoreType.DMA
    tiles, units = pl.pallas_call(
        kernel,
        out_shape=(
            jax.ShapeDtypeStruct((64, 2 * PB, LANES), BF16),
            jax.ShapeDtypeStruct((64, 1, LANES), F32),
        ),
        in_specs=[
            pl.BlockSpec(memory_space=pl.ANY),
            pl.BlockSpec(memory_space=pltpu.VMEM),
            pl.BlockSpec(memory_space=pl.ANY),
            pl.BlockSpec(memory_space=pl.ANY),
            pl.BlockSpec(memory_space=pltpu.VMEM),
        ],
        out_specs=(pl.BlockSpec(memory_space=pl.ANY), pl.BlockSpec(memory_space=pl.ANY)),
        scratch_shapes=[
            pltpu.VMEM((GROUP, 16, 512), F32),
            pltpu.VMEM((2, 64, PB, LANES), F32),
            pltpu.VMEM((2, 2, 4, 8, PB, LANES), F32),
            pltpu.VMEM((SLAB, PB, HALF), F32),
            pltpu.VMEM((SLAB, PB, HALF), F32),
            pltpu.VMEM((SLAB, PB, HALF), F32),
            pltpu.VMEM((STEPS, SLAB * PB, HALF), BF16),
            pltpu.VMEM((STEPS, SLAB * PB, HALF), BF16),
            pltpu.VMEM((STEPS, 2, HALO, PB, HALF), F32),
            pltpu.VMEM((2, 32, GROUP, 1024), BF16),
            pltpu.VMEM((2, 1024, HALF), BF16),
            pltpu.VMEM((SLAB * PB, HALF), F32),
            pltpu.VMEM((SLAB * PB, HALF), F32),
            pltpu.VMEM((4, 8, LANES), F32),
            pltpu.VMEM((2, 16, 512), F32),
            pltpu.VMEM((LANES, LANES), F32),
            pltpu.VMEM((SLAB, PB, LANES), F32),
            pltpu.VMEM((2, 8, 4, 2 * PB, LANES), BF16),
            pltpu.VMEM((2, 1, LANES), F32),
            dma, dma((2,)), dma((2,)), dma((2,)), dma((STEPS, 2)), dma((STEPS, 2)),
            dma((6,)), dma((6,)), dma((2,)), dma, dma, dma, dma, pltpu.SemaphoreType.REGULAR,
        ],
        compiler_params=pltpu.CompilerParams(collective_id=0, has_side_effects=True),
        name="boltzmann",
    )(
        distribution,
        courant.reshape(8, LANES),
        gain_matrix.reshape(32, 2, GROUP, 1024),
        product_matrix.reshape(32, 2, GROUP, 1024),
        collision_rate,
    )
    return pl.pallas_call(
        place,
        out_shape=jax.ShapeDtypeStruct((GROUP, 16, 512), F32),
        in_specs=[pl.BlockSpec(memory_space=pltpu.VMEM)] * 2,
        out_specs=pl.BlockSpec(memory_space=pltpu.VMEM),
        name="place",
    )(tiles, units)


def solution(mesh):
    in_specs = (P("vel", "space", None), P(), P(), P(), P("space", None))
    out_specs = P("vel", "space", None)
    return jax.shard_map(body, mesh=mesh, in_specs=in_specs, out_specs=out_specs, check_vma=False)
```

```python
import functools

import jax
import jax.numpy as jnp
from jax import lax
from jax.experimental import pallas as pl
from jax.experimental.pallas import tpu as pltpu
from jax.sharding import PartitionSpec as P

STEPS = 2
TIME_STEP = 0.2
MESH = pl.DeviceIdType.MESH
F32 = jnp.float32
BF16 = jnp.bfloat16
RING = 8
LANES = 128
GROUP = 16
PB = 8
SLAB = 32
HALO = 4
SPAN = 2.0 ** 30
HALF = 512

OFFSETS = sorted(
    [(dx, dz) for dx in range(RING) for dz in range(RING) if (dx, dz) != (0, 0)],
    key=lambda o: -(min(o[0], RING - o[0]) + min(o[1], RING - o[1])),
)


def coords():
    vel, space = lax.axis_index("vel"), lax.axis_index("space")
    z_hi, x, core = vel // 16, (vel // 2) % 8, vel % 2
    y, z_lo = space // 2, space % 2
    return x, y, z_hi, z_lo, core


def device(x, y, z, core):
    return {"vel": (z // 2) * 16 + x * 2 + core, "space": y * 2 + z % 2}


def swap_groups(tiles):
    lane = lax.broadcasted_iota(jnp.int32, (8, LANES), 1) // GROUP
    tiles = list(tiles)
    for bit in (4, 2, 1):
        low = (lane & bit) == 0
        for i in range(8):
            if i & bit:
                continue
            j = i | bit
            a, b = tiles[i], tiles[j]
            tiles[i] = jnp.where(low, a, pltpu.roll(b, bit * GROUP, 1))
            tiles[j] = jnp.where(low, pltpu.roll(a, LANES - bit * GROUP, 1), b)
    return tiles


def encode(values):
    square = values * values
    power = square * square
    return jnp.where(values < 0.0, -power, power)


def decode(powers):
    root = jnp.sqrt(jnp.sqrt(jnp.abs(powers)))
    return jnp.where(powers < 0.0, -root, root)


def sweep(values, speed, rising, reach):
    n = len(values)
    differ = [values[i + 1] - values[i] for i in range(n - 1)]
    slopes = [None] + [
        jnp.maximum(
            jnp.minimum(differ[i], jnp.maximum(differ[i - 1], 0.0)),
            jnp.minimum(differ[i - 1], 0.0),
        )
        for i in range(1, n - 1)
    ]
    fluxes = {}
    for i in range(1, n - 2):
        value = jnp.where(rising, values[i], values[i + 1])
        slope = jnp.where(rising, slopes[i], slopes[i + 1])
        fluxes[i] = speed * (value + reach * slope)
    return {i: fluxes[i] - fluxes[i - 1] for i in range(2, n - 2)}


def kernel(
    dist_ref, cour_ref, gain_ref, prod_ref, rate_ref, out_ref, unit_ref,
    sin, send, recv, state, later, smooth, ownr, parr, halo, raw, turned, first, second,
    cour, rates, rate_cols, rate_b, sout, sunit,
    in_sem, mat_sem, a2a_ss, a2a_rs, halo_ss, halo_rs, core_ss, core_rs,
    rate_sem, out_ss, out_rs, unit_ss, unit_rs, gone,
):
    x, y, z_hi, z_lo, core = coords()
    z = z_hi * 2 + z_lo
    block = x * RING + z
    up_dev = device(x, lax.rem(y + 1, RING), z, core)
    down_dev = device(x, lax.rem(y + RING - 1, RING), z, core)
    twin = device(x, y, z, 1 - core)
    level = device(x, y, z_hi * 2 + 1 - z_lo, core)

    turn = 1 - 2 * core

    def far(o):
        return lax.rem(x + RING + turn * o[0], RING), lax.rem(z + RING + turn * o[1], RING)

    barrier = pltpu.get_barrier_semaphore()
    for o in OFFSETS:
        xx, zz = far(o)
        pl.semaphore_signal(barrier, 1, device_id=device(xx, y, zz, core), device_id_type=MESH)
    for peer in (up_dev, down_dev, twin):
        pl.semaphore_signal(barrier, 1, device_id=peer, device_id_type=MESH)

    load = pltpu.make_async_copy(dist_ref, sin, in_sem)
    load.start()
    mats = [
        pltpu.make_async_copy(gain_ref.at[:, core], raw.at[0], mat_sem.at[0]),
        pltpu.make_async_copy(prod_ref.at[:, core], raw.at[1], mat_sem.at[1]),
    ]
    for m in mats:
        m.start()
    load.wait()

    for h in range(2):
        for q in range(4):
            rows = jnp.concatenate(
                [sin[:, h * 8 + i, q * LANES:(q + 1) * LANES] for i in range(8)], axis=0
            )
            send[h, q * 16:(q + 1) * 16] = rows.T.reshape(16, PB, LANES)

    pl.semaphore_wait(barrier, len(OFFSETS) + 3)

    rate_copy = pltpu.make_async_remote_copy(
        rate_ref, rates.at[z_lo], rate_sem.at[0], rate_sem.at[1], device_id=level, device_id_type=MESH
    )
    def send_phase(phase):
        h = z_lo if phase == 0 else 1 - z_lo
        for o in OFFSETS:
            xx, zz = far(o)
            pltpu.make_async_remote_copy(
                send.at[h, xx * RING + zz], recv.at[phase, z_lo, z_hi, x],
                a2a_ss.at[phase], a2a_rs.at[phase],
                device_id=device(xx, y, zz, core), device_id_type=MESH,
            ).start()
        pltpu.make_async_copy(
            send.at[h, block], recv.at[phase, z_lo, z_hi, x], a2a_rs.at[phase]
        ).start()

    rate_copy.start()
    send_phase(0)

    speeds = cour_ref[...]
    lane = lax.broadcasted_iota(jnp.int32, (8, LANES), 1)
    even = jnp.zeros((8, LANES), F32)
    odd = jnp.zeros((8, LANES), F32)
    for i in range(4):
        for is_odd in range(2):
            target = (is_odd * 4 + i) * GROUP
            shifts = [(target - i * 32 - cc * GROUP) % LANES for cc in range(2)]
            rolled = [pltpu.roll(speeds, s, 1) if s else speeds for s in shifts]
            here = (lane // GROUP) == (is_odd * 4 + i)
            piece = jnp.where(core == 0, rolled[0], rolled[1])
            if is_odd:
                odd = jnp.where(here, piece, odd)
            else:
                even = jnp.where(here, piece, even)
    for t in range(4):
        cour[t] = jnp.where(lane < 64, even[2 * t:2 * t + 1], odd[2 * t + 1:2 * t + 2])

    m_at = lax.broadcasted_iota(jnp.int32, (256, 256), 0)
    n_at = lax.broadcasted_iota(jnp.int32, (256, 256), 1)
    whose = jnp.where(m_at < LANES, core, 1 - core)
    inner = m_at % LANES
    pick = (n_at == (inner // GROUP) * 32 + whose * GROUP + inner % GROUP).astype(F32).astype(BF16)
    for k in range(2):
        mats[k].wait()
        for b in range(4):
            block_cols = raw[k, :, :, b * 256:(b + 1) * 256].reshape(HALF, 256)
            res = lax.dot_general(
                pick, block_cols, (((1,), (1,)), ((), ())), preferred_element_type=F32
            ).astype(BF16)
            turned[k, b * LANES:(b + 1) * LANES] = res[:LANES]
            turned[k, HALF + b * LANES:HALF + (b + 1) * LANES] = res[LANES:]

    def spread_rates():
        rates[z_lo] = rate_ref[...]
        rate_copy.wait()
        rate_cols[...] = jnp.zeros_like(rate_cols)
        cell_tile = pl.multiple_of((block // 16) * LANES, LANES)
        rate_cols[0:16] = rates[0, :, pl.ds(cell_tile, LANES)]
        rate_cols[16:32] = rates[1, :, pl.ds(cell_tile, LANES)]
        rate_cols[...] = rate_cols[...].T
        column = rate_cols[pl.ds(pl.multiple_of((block % 16) * PB, PB), PB), :]
        for i in range(SLAB):
            rate_b[i] = jnp.broadcast_to(column[:, i:i + 1], (PB, LANES))

    sent = send.at[0, pl.ds(0, len(OFFSETS))]
    pltpu.make_async_copy(sent, sent, a2a_ss.at[0]).wait()
    pl.semaphore_signal(gone, 1, device_id=twin, device_id_type=MESH)
    pl.semaphore_wait(gone, 1)
    send_phase(1)

    def arrived(phase):
        pltpu.make_async_copy(recv.at[phase], recv.at[phase], a2a_rs.at[phase]).wait()

    def unpack(phase):
        for zl in range(2):
            h = zl if phase == 0 else 1 - zl
            for t in range(4):
                tiles = swap_groups([recv[phase, zl, t, g] for g in range(8)])
                for i in range(8):
                    state[zl * 16 + h * 8 + i, :, t * LANES:(t + 1) * LANES] = tiles[i]

    def send_faces(source, step):
        copies = [
            pltpu.make_async_remote_copy(
                source.at[pl.ds(SLAB - HALO, HALO)], halo.at[step, 0], halo_ss.at[step, 0],
                halo_rs.at[step, 0], device_id=up_dev, device_id_type=MESH,
            ),
            pltpu.make_async_remote_copy(
                source.at[pl.ds(0, HALO)], halo.at[step, 1], halo_ss.at[step, 1],
                halo_rs.at[step, 1], device_id=down_dev, device_id_type=MESH,
            ),
        ]
        for c in copies:
            c.start()
        return copies

    def advect(source, step, lo, count):
        for t in range(4):
            cols = slice(t * LANES, (t + 1) * LANES)
            c = cour[t]
            rising = c > 0.0
            reach = jnp.where(rising, 0.5 * (1.0 - c), -(0.5 * (1.0 + c)))
            planes = []
            for i in range(lo - HALO, lo + count + HALO):
                if i < 0:
                    planes.append(halo[step, 0, i + HALO, :, cols])
                elif i >= SLAB:
                    planes.append(halo[step, 1, i - SLAB, :, cols])
                else:
                    planes.append(source[i, :, cols])
            less = sweep(planes, c, rising, reach)
            section = [planes[i] - less[i] for i in range(2, len(planes) - 2)]
            less2 = sweep(section, c, rising, reach)
            result = [
                0.5 * planes[i + 2] + 0.5 * (section[i] - less2[i])
                for i in range(2, len(section) - 2)
            ]
            for i in range(0, count, 2):
                smooth[lo + i, :, cols] = result[i]
                smooth[lo + i + 1, :, cols] = result[i + 1]
                pair = jnp.concatenate([result[i], result[i + 1]], axis=0)
                ownr[step, (lo + i) * PB:(lo + i + 2) * PB, cols] = pair.astype(BF16)

    def share(step, number, lo, count):
        rows = pl.ds(lo * PB, count * PB)
        copy = pltpu.make_async_remote_copy(
            ownr.at[step, rows], parr.at[step, rows], core_ss.at[number], core_rs.at[number],
            device_id=twin, device_id_type=MESH,
        )
        copy.start()
        return copy

    def rows_of(ref, step, ranges):
        parts = [ref[step, lo * PB:(lo + count) * PB] for lo, count in ranges]
        return parts[0] if len(parts) == 1 else jnp.concatenate(parts, axis=0)

    def products(source, step, ranges, half, add):
        block_rows = rows_of(source, step, ranges)
        for k, total in ((0, first), (1, second)):
            value = jnp.dot(
                block_rows, turned[k, half * HALF:(half + 1) * HALF], preferred_element_type=F32
            )
            at = 0
            for lo, count in ranges:
                rows = slice(lo * PB, (lo + count) * PB)
                part = value[at:at + count * PB]
                total[rows] = total[rows] + part if add else part
                at += count * PB

    def update(target, step, ranges):
        for lo, count in ranges:
            for i in range(lo, lo + count, 2):
                rows = slice(i * PB, (i + 2) * PB)
                gained = (first[rows] * second[rows]).astype(BF16).astype(F32)
                rounded = ownr[step, rows].astype(F32)
                for j in range(2):
                    part = slice(j * PB, (j + 1) * PB)
                    rate = jnp.concatenate([rate_b[i + j]] * 4, axis=1)
                    target[i + j] = smooth[i + j] + TIME_STEP * (
                        gained[part] - rate * rounded[part]
                    )

    arrived(0)
    unpack(0)
    faces = send_faces(state, 0)
    spread_rates()
    for c in faces:
        c.wait()
    edges = ((0, HALO), (SLAB - HALO, HALO))
    shares = []
    for n, (lo, count) in enumerate(edges):
        advect(state, 0, lo, count)
        shares.append(share(0, n, lo, count))
    products(ownr, 0, edges, 0, False)
    for c in shares:
        c.wait()
    products(parr, 0, edges, 1, True)
    update(later, 0, edges)
    faces = send_faces(later, 1)
    arrived(1)
    unpack(1)
    inside = ((HALO, 12), (HALO + 12, 12))
    shares = []
    for n, (lo, count) in enumerate(inside):
        advect(state, 0, lo, count)
        shares.append(share(0, 2 + n, lo, count))
    inside = ((HALO, 24),)
    products(ownr, 0, inside, 0, False)
    for c in shares:
        c.wait()
    products(parr, 0, inside, 1, True)
    update(later, 0, inside)
    for c in faces:
        c.wait()

    def dispatch(z_to):
        t, zl = z_to // 2, z_to % 2
        for dx in (4, 3, 5, 2, 6, 1, 7, 0):
            xx = lax.rem(x + RING + turn * dx, RING)

            def remote():
                to = device(xx, y, z_to, core)
                pltpu.make_async_remote_copy(
                    sunit.at[zl], unit_ref.at[block], unit_ss, unit_rs,
                    device_id=to, device_id_type=MESH,
                ).start()
                pltpu.make_async_remote_copy(
                    sout.at[zl, xx, t], out_ref.at[block], out_ss, out_rs,
                    device_id=to, device_id_type=MESH,
                ).start()

            if dx:
                remote()
            else:
                pl.when(z != z_to)(remote)

                @pl.when(z == z_to)
                def _():
                    pltpu.make_async_copy(sunit.at[zl], unit_ref.at[block], unit_rs).start()
                    pltpu.make_async_copy(sout.at[zl, x, t], out_ref.at[block], out_rs).start()

    shares = []
    for zl in range(2):
        advect(later, 1, zl * 16, 16)
        shares.append(share(1, 4 + zl, zl * 16, 16))
    for zl in range(2):
        part = ((zl * 16, 16),)
        products(ownr, 1, part, 0, False)
        shares[zl].wait()
        products(parr, 1, part, 1, True)
        update(state, 1, part)
        top = jnp.abs(state[zl * 16])
        for i in range(1, 16):
            top = jnp.maximum(top, jnp.abs(state[zl * 16 + i]))
        top = jnp.maximum(jnp.max(top, axis=(0, 1), keepdims=True), 1e-20)
        unit = jnp.broadcast_to(top * (1.0 / SPAN), (PB, LANES)).astype(BF16).astype(F32)
        sunit[zl] = unit[:1]
        scale = 1.0 / unit
        for t in range(4):
            pair = [
                swap_groups(
                    [
                        encode(state[zl * 16 + h * 8 + i, :, t * LANES:(t + 1) * LANES] * scale)
                        for i in range(8)
                    ]
                )
                for h in range(2)
            ]
            for g in range(8):
                sout[zl, g, t] = jnp.concatenate([pair[0][g], pair[1][g]], axis=0).astype(BF16)
        dispatch(zl)
    for z_to in range(2, RING):
        dispatch(z_to)

    pltpu.make_async_copy(out_ref, out_ref, out_rs).wait()
    pltpu.make_async_copy(unit_ref, unit_ref, unit_rs).wait()
    sent = out_ref.at[pl.ds(0, len(OFFSETS))]
    pltpu.make_async_copy(sent, sent, out_ss).wait()
    sent = unit_ref.at[pl.ds(0, len(OFFSETS))]
    pltpu.make_async_copy(sent, sent, unit_ss).wait()
    sent = send.at[0, pl.ds(0, len(OFFSETS))]
    pltpu.make_async_copy(sent, sent, a2a_ss.at[1]).wait()


def place(tiles_ref, unit_ref, out_ref):
    m_at = lax.broadcasted_iota(jnp.int32, (LANES, LANES), 0)
    n_at = lax.broadcasted_iota(jnp.int32, (LANES, LANES), 1)
    order = (n_at == (m_at % 8) * GROUP + m_at // 8).astype(F32).astype(BF16)
    last = (((1,), (1,)), ((), ()))
    for q in range(4):
        part = slice(q * 16, (q + 1) * 16)
        cols = slice(q * LANES, (q + 1) * LANES)
        units = jnp.broadcast_to(unit_ref[part], (16, PB, LANES)).reshape(LANES, LANES).astype(BF16)
        unit = lax.dot_general(order[:8], units, last, preferred_element_type=F32)
        tiles = tiles_ref[part].astype(F32)
        for h in range(2):
            block = tiles[:, h * PB:(h + 1) * PB].reshape(LANES, LANES).astype(BF16)
            rows = lax.dot_general(order, block, last, preferred_element_type=F32)
            out_ref[:, h * 8:(h + 1) * 8, cols] = decode(rows).reshape(GROUP, 8, LANES) * unit


def body(distribution, courant, gain_matrix, product_matrix, collision_rate):
    dma = pltpu.SemaphoreType.DMA
    tiles, units = pl.pallas_call(
        kernel,
        out_shape=(
            jax.ShapeDtypeStruct((64, 2 * PB, LANES), BF16),
            jax.ShapeDtypeStruct((64, 1, LANES), F32),
        ),
        in_specs=[
            pl.BlockSpec(memory_space=pl.ANY),
            pl.BlockSpec(memory_space=pltpu.VMEM),
            pl.BlockSpec(memory_space=pl.ANY),
            pl.BlockSpec(memory_space=pl.ANY),
            pl.BlockSpec(memory_space=pltpu.VMEM),
        ],
        out_specs=(pl.BlockSpec(memory_space=pl.ANY), pl.BlockSpec(memory_space=pl.ANY)),
        scratch_shapes=[
            pltpu.VMEM((GROUP, 16, 512), F32),
            pltpu.VMEM((2, 64, PB, LANES), F32),
            pltpu.VMEM((2, 2, 4, 8, PB, LANES), F32),
            pltpu.VMEM((SLAB, PB, HALF), F32),
            pltpu.VMEM((SLAB, PB, HALF), F32),
            pltpu.VMEM((SLAB, PB, HALF), F32),
            pltpu.VMEM((STEPS, SLAB * PB, HALF), BF16),
            pltpu.VMEM((STEPS, SLAB * PB, HALF), BF16),
            pltpu.VMEM((STEPS, 2, HALO, PB, HALF), F32),
            pltpu.VMEM((2, 32, GROUP, 1024), BF16),
            pltpu.VMEM((2, 1024, HALF), BF16),
            pltpu.VMEM((SLAB * PB, HALF), F32),
            pltpu.VMEM((SLAB * PB, HALF), F32),
            pltpu.VMEM((4, 8, LANES), F32),
            pltpu.VMEM((2, 16, 512), F32),
            pltpu.VMEM((LANES, LANES), F32),
            pltpu.VMEM((SLAB, PB, LANES), F32),
            pltpu.VMEM((2, 8, 4, 2 * PB, LANES), BF16),
            pltpu.VMEM((2, 1, LANES), F32),
            dma, dma((2,)), dma((2,)), dma((2,)), dma((STEPS, 2)), dma((STEPS, 2)),
            dma((6,)), dma((6,)), dma((2,)), dma, dma, dma, dma, pltpu.SemaphoreType.REGULAR,
        ],
        compiler_params=pltpu.CompilerParams(collective_id=0, has_side_effects=True),
        name="boltzmann",
    )(
        distribution,
        courant.reshape(8, LANES),
        gain_matrix.reshape(32, 2, GROUP, 1024),
        product_matrix.reshape(32, 2, GROUP, 1024),
        collision_rate,
    )
    return pl.pallas_call(
        place,
        out_shape=jax.ShapeDtypeStruct((GROUP, 16, 512), F32),
        in_specs=[pl.BlockSpec(memory_space=pltpu.VMEM)] * 2,
        out_specs=pl.BlockSpec(memory_space=pltpu.VMEM),
        name="place",
    )(tiles, units)


def solution(mesh):
    in_specs = (P("vel", "space", None), P(), P(), P(), P("space", None))
    out_specs = P("vel", "space", None)
    return jax.shard_map(body, mesh=mesh, in_specs=in_specs, out_specs=out_specs, check_vma=False)
```
